32 devices in a mesh: dom: 16 (over z, y, core), sub: 2 (over x).
Axes of the slice: x: 2, y: 2, z: 4, core: 2. Of those that a mesh axis runs over, the one named last changes fastest.
Arguments:
- dofs: float32 [9, 56, 512], P(None, None, ('dom', 'sub')), may hold values from -6 to 6
- stiffness: float32 [3, 56, 56], replicated, may hold values from -0.75 to 0.75
- projection: float32 [4, 21, 56], replicated, may hold values from -0.75 to 0.75
- star: float32 [3, 9, 9, 512], P(None, None, None, ('dom', 'sub')), may hold values from -1.25 to 1.25
- flux_minus: float32 [4, 9, 9, 512], P(None, None, None, ('dom', 'sub')), may hold values from -1 to 1
- flux_plus: float32 [4, 9, 9, 512], P(None, None, None, ('dom', 'sub')), may hold values from -1 to 1
- fault_flux: float32 [9, 9], replicated, may hold values from -2 to 2
- fault_faces: int32 [4, 512], P(None, ('dom', 'sub')), may hold values 0 or 1
- levels: int32 [512], P(('dom', 'sub')), may hold values from 0 to 1, as said below
- face_source: int32 [4, 512], P(None, ('dom', 'sub')), may hold values from 0 to 87, as said below
- send_source: int32 [128], P(('dom', 'sub')), may hold values from 0 to 63
Outputs:
- dofs_after: float32 [9, 56, 512], P(None, None, ('dom', 'sub'))
The draws below stay inside these ranges and needn't reach their ends.
Inputs may be any that keep to these rules, and one draw needn't show every extreme that they name: `levels`: on every device at most 8 of its 16 elements have level 0, and some device has exactly 8. `face_source`: values below 64 name a face of the same device as face times 16 plus element; larger values name received exported faces as defined in the reference program.
All inputs are finite; a program needn't handle non-finite values. No bound on the sum of `fault_faces` on one device may be relied on, other than what follows from the above.
Results may differ from the reference program's by a relative error of at most 0.0001.
Values sent between devices are 32-bit elements; how exact they have to be, the bound alone decides.
No kernel may reach another device: no remote copies, remote signals or barrier semaphores. Data moves between devices by JAX's collectives and lax.ppermute only.
A program may use at most 64 MiB of HBM per device.

```python
import math
import jax
import jax.numpy as jnp
from jax import lax

VARS = 9
MODES = 56
FACE_MODES = 21
ORDER = 6
E_DEV = 16
SEND = 4
FINE_MOST = 8
RECV = 24
ELEMS = 512
N_DOM = 16
N_SUB = 2
DEVICES = 32


def draw_levels(key, part):
    device_count = ELEMS // E_DEV
    key_count, key_busiest, key_ranks = jax.random.split(key, 3)
    counts = jax.random.randint(key_count, (device_count,), FINE_MOST // 4, FINE_MOST + 1)
    busiest = jax.random.randint(key_busiest, (), 0, device_count)
    counts = jnp.where(jnp.arange(device_count) == busiest, FINE_MOST, counts)
    ranks = jax.vmap(lambda single: jax.random.permutation(single, E_DEV))(jax.random.split(key_ranks, device_count))
    return jnp.where(ranks < counts[:, None], 0, 1).astype(jnp.int32).reshape(-1)


def draw_face_source(key, part):
    key_kind, key_local, key_remote = jax.random.split(key, 3)
    grid_shape = (4, ELEMS)
    choose_kind = jax.random.randint(key_kind, grid_shape, 0, 4)
    local_codes = jax.random.randint(key_local, grid_shape, 0, 4 * E_DEV)
    remote_codes = 4 * E_DEV + jax.random.randint(key_remote, grid_shape, 0, RECV)
    return jnp.where(choose_kind < 3, local_codes, remote_codes).astype(jnp.int32)


def touch_ends(result, key, least, high):
    extent = result.shape
    index_at = [jax.random.randint(jax.random.fold_in(key, axis), (), 0, extent[axis]) for axis in range(len(extent))]
    result = result.at[tuple(index_at)].set(least)
    longest = extent.index(max(extent))
    index_at[longest] = (index_at[longest] + 1) % extent[longest]
    return result.at[tuple(index_at)].set(high)


def block_scale(key, shape, cuts, least, largest):
    gain = 1.0
    for dim, blocks in cuts:
        heights = jax.random.uniform(jax.random.fold_in(jax.random.fold_in(key, 6), dim), (blocks,), jnp.float32, least / len(cuts), largest / len(cuts))
        gain = gain * jnp.repeat(jnp.exp(heights), shape[dim] // blocks).reshape((-1,) + (1,) * (len(shape) - 1 - dim))
    return gain


def bell_draw(stream_key, extent, width, most, cuts=(), kind=jnp.bfloat16):
    values = width * jax.random.normal(stream_key, extent, jnp.float32)
    if cuts:
        values = values * block_scale(stream_key, extent, cuts, -0.22, 0.18)
    return jnp.clip(values, -most, most).astype(kind)


def setup_inputs(seed: int = 0) -> dict:
    arg_keys = jax.random.split(jax.random.key(seed), 12)
    dofs = bell_draw(arg_keys[0], (VARS, MODES, ELEMS), 1.0, 6.0, ((2, 32),), jnp.float32)
    stiffness = bell_draw(arg_keys[1], (3, MODES, MODES), MODES ** -0.5, 0.75, (), jnp.float32)
    projection = bell_draw(arg_keys[2], (4, FACE_MODES, MODES), MODES ** -0.5, 0.75, (), jnp.float32)
    star = bell_draw(arg_keys[3], (3, VARS, VARS, ELEMS), 27 ** -0.5, 1.25, ((3, 32),), jnp.float32)
    flux_minus = bell_draw(arg_keys[4], (4, VARS, VARS, ELEMS), 36 ** -0.5, 1.0, ((3, 32),), jnp.float32)
    flux_plus = bell_draw(arg_keys[5], (4, VARS, VARS, ELEMS), 36 ** -0.5, 1.0, ((3, 32),), jnp.float32)
    fault_flux = bell_draw(arg_keys[6], (VARS, VARS), 9 ** -0.5, 2.0, (), jnp.float32)
    fault_faces = touch_ends((jax.random.randint(arg_keys[7], (4, ELEMS), 0, 8) < 1).astype(jnp.int32), jax.random.fold_in(arg_keys[7], 1), 0, 1)
    levels = draw_levels(jax.random.fold_in(arg_keys[11], 71), 0)
    face_source = draw_face_source(jax.random.fold_in(arg_keys[11], 71), 0)
    send_source = touch_ends(jax.random.randint(arg_keys[10], (SEND * DEVICES,), 0, 4 * E_DEV), jax.random.fold_in(arg_keys[10], 1), 0, (4 * E_DEV) - 1).astype(jnp.int32)
    return dict(dofs=dofs, stiffness=stiffness, projection=projection, star=star, flux_minus=flux_minus, flux_plus=flux_plus, fault_flux=fault_flux, fault_faces=fault_faces, levels=levels, face_source=face_source, send_source=send_source)


fine_step = 0.75
exact_reference = lax.Precision.HIGHEST


def taylor_weights(start_time, stop_time, term_count):
    return [(stop_time ** (term + 1) - start_time ** (term + 1)) / math.factorial(term + 1) for term in range(term_count)]


def derivatives(state_now, stiffness, star_contribution):
    taylor_series = [state_now]
    for repeat in range(ORDER - 1):
        time_slopes = jnp.einsum("dmn,wne->dwme", stiffness, taylor_series[-1], precision=exact_reference)
        taylor_series.append(jnp.einsum("usij,uifj->sfj", star_contribution, time_slopes, precision=exact_reference))
    return jnp.stack(taylor_series)


def integrate(taylor_series, start_time, stop_time):
    quadrature_weights = jnp.array(taylor_weights(start_time, stop_time, taylor_series.shape[0]), jnp.float32)
    return jnp.einsum("h,hlui->lui", quadrature_weights, taylor_series, precision=exact_reference)


def face_values(field_state, projection):
    return jnp.einsum("bly,qyp->qlbp", projection, field_state, precision=exact_reference)


def advance(state_now, own_part, own_faces, beside, stiffness, projection, star_contribution, minus_part, coupling_part):
    incoming_flux = jnp.einsum("dvwe,wne->dvne", star_contribution, own_part, precision=exact_reference)
    volume_term = jnp.einsum("utx,uytz->yxz", stiffness, incoming_flux, precision=exact_reference)
    flux_terms = jnp.einsum("fvwe,wjfe->vjfe", minus_part, own_faces, precision=exact_reference)
    flux_terms = flux_terms + jnp.einsum("fvwe,wjfe->vjfe", coupling_part, beside, precision=exact_reference)
    surface_term = jnp.einsum("alz,qlad->qzd", projection, flux_terms, precision=exact_reference)
    return state_now + volume_term - surface_term


def to_blocks(array):
    split = array.reshape(array.shape[:-1] + (ELEMS // E_DEV, E_DEV))
    return jnp.moveaxis(split, -2, 0)


def from_blocks(array):
    joined = jnp.moveaxis(array, 0, -2)
    return joined.reshape(joined.shape[:-2] + (ELEMS,))


def reference(dofs, stiffness, projection, star, flux_minus, flux_plus, fault_flux, fault_faces, levels, face_source, send_source):
    device_count = ELEMS // E_DEV
    coupling = jnp.where(fault_faces[:, None, None, :] == 1, fault_flux[None, :, :, None], flux_plus)
    element_ids = jnp.arange(ELEMS, dtype=jnp.int32)
    device_ids = (element_ids // E_DEV)[None, :]
    local_column = device_ids * (4 * E_DEV) + face_source
    offset = face_source - 4 * E_DEV
    side_index = offset // (N_SUB * SEND)
    sub_index = (offset // SEND) % N_SUB
    slot_index = offset % SEND
    source_device = ((device_ids // N_SUB + side_index - 1) % N_DOM) * N_SUB + sub_index
    send_position = jnp.clip(source_device * SEND + slot_index, 0, device_count * SEND - 1).astype(jnp.int32)
    remote_column = source_device * (4 * E_DEV) + send_source[send_position]
    column = jnp.where(face_source < 4 * E_DEV, local_column, remote_column).astype(jnp.int32)
    column_order = to_blocks(column).reshape(-1)

    def beside_values(face_blocks):
        source_table = jnp.moveaxis(face_blocks, 0, 2).reshape(VARS * FACE_MODES, -1)
        picked = jnp.take(source_table, column_order, axis=1)
        return jnp.moveaxis(picked.reshape(VARS, FACE_MODES, device_count, 4, E_DEV), 2, 0)

    block_dofs = to_blocks(dofs)
    block_star = to_blocks(star)
    block_minus = to_blocks(flux_minus)
    block_coupling = to_blocks(coupling)
    block_fine = to_blocks(levels == 0)

    def phase_one(items):
        state_now, star_contribution = items
        taylor_series = derivatives(state_now, stiffness, star_contribution)
        first_half = integrate(taylor_series, 0.0, fine_step)
        second_half = integrate(taylor_series, fine_step, 2.0 * fine_step)
        return first_half, second_half, face_values(first_half, projection)

    first_b, second_b, first_faces_b = lax.map(phase_one, (block_dofs, block_star))
    beside_first_b = beside_values(first_faces_b)

    def phase_two(items):
        state_now, star_contribution, minus_part, coupling_part, is_fine, first_half, second_half, first_faces, beside_first = items
        updated = advance(state_now, first_half, first_faces, beside_first, stiffness, projection, star_contribution, minus_part, coupling_part)
        state_one = jnp.where(is_fine, updated, state_now)
        fine_integral = integrate(derivatives(state_one, stiffness, star_contribution), 0.0, fine_step)
        carried = jnp.where(is_fine, fine_integral, second_half)
        return state_one, carried, face_values(carried, projection)

    state_one_b, carried_b, carried_faces_b = lax.map(phase_two, (block_dofs, block_star, block_minus, block_coupling, block_fine, first_b, second_b, first_faces_b, beside_first_b))
    beside_carried_b = beside_values(carried_faces_b)

    def phase_three(items):
        state_now, star_contribution, minus_part, coupling_part, is_fine, first_half, second_half, beside_first, state_one, carried, carried_faces, beside_carried = items
        fine_new = advance(state_one, carried, carried_faces, beside_carried, stiffness, projection, star_contribution, minus_part, coupling_part)
        whole_step = first_half + second_half
        coarse_new = advance(state_now, whole_step, face_values(whole_step, projection), beside_first + beside_carried, stiffness, projection, star_contribution, minus_part, coupling_part)
        return jnp.where(is_fine, fine_new, coarse_new)

    result_b = lax.map(phase_three, (block_dofs, block_star, block_minus, block_coupling, block_fine, first_b, second_b, beside_first_b, state_one_b, carried_b, carried_faces_b, beside_carried_b))
    return from_blocks(result_b)
```

```python
import math

import jax
import jax.numpy as jnp
from jax import lax
from jax.experimental import pallas as pl
from jax.experimental.pallas import tpu as pltpu
from jax.sharding import PartitionSpec as P

ORDER = 6

fine_step = 0.75
f32 = jnp.float32
bf16 = jnp.bfloat16


def taylor_weights(start_time, stop_time, term_count):
    return [
        (stop_time ** (term + 1) - start_time ** (term + 1)) / math.factorial(term + 1)
        for term in range(term_count)
    ]


def mm(a, b):
    return jnp.dot(a, b, preferred_element_type=f32)


def halves(x):
    hi = x.astype(bf16).astype(f32)
    return hi, x - hi


def left_form(a):
    hi, lo = halves(a)
    return jnp.concatenate([hi, hi, lo], axis=1).astype(bf16)


def left(form, x):
    hi, lo = halves(x)
    return mm(form, jnp.concatenate([hi, lo, hi], axis=0).astype(bf16))


def right(x, b_hi, b_lo):
    rows = x.shape[0]
    hi, lo = halves(x)
    both = mm(jnp.concatenate([hi, lo], axis=0).astype(bf16), b_hi)
    return both[:rows] + both[rows:] + mm(hi.astype(bf16), b_lo)


def stiff_rows(stiff_ref, flip):
    mats = [stiff_ref[d] for d in range(stiff_ref.shape[0])]
    return jnp.concatenate([m.T if flip else m for m in mats], axis=0)


def face_pad(face_modes):
    return -(-face_modes // 8) * 8


def face_rows(proj_ref):
    faces, width, modes = proj_ref.shape
    gap = face_pad(width) - width
    parts = []
    for f in range(faces):
        block = proj_ref[f]
        if gap:
            block = jnp.concatenate([block, jnp.zeros((gap, modes), f32)], axis=0)
        parts.append(block)
    return jnp.concatenate(parts, axis=0)


def star_apply(form, x, bh_ref, bl_ref):
    t = left(form, x)
    rows = x.shape[0]
    out = None
    for d in range(bh_ref.shape[0]):
        term = right(t[d * rows : (d + 1) * rows], bh_ref[d], bl_ref[d])
        out = term if out is None else out + term
    return out


def series(form, x, bh_ref, bl_ref, weight_lists):
    sums = [x * f32(ws[0]) for ws in weight_lists]
    for k in range(1, ORDER):
        x = star_apply(form, x, bh_ref, bl_ref)
        sums = [s + x * f32(ws[k]) for s, ws in zip(sums, weight_lists)]
    return sums


def export_rows(faces_all, send_ref, out_ref, var_count, elem_count, face_count):
    slots = send_ref.shape[0]
    cols = var_count * slots
    rows = var_count * elem_count
    width = faces_all.shape[0] // face_count
    row = lax.broadcasted_iota(jnp.int32, (rows, cols), 0)
    col = lax.broadcasted_iota(jnp.int32, (rows, cols), 1)
    row_v, row_e = row // elem_count, row % elem_count
    col_v, col_s = col // slots, col % slots
    code = jnp.zeros((rows, cols), jnp.int32)
    for s in range(slots):
        code = jnp.where(col_s == s, send_ref[s], code)
    same = row_v == col_v
    hi, lo = halves(faces_all)
    mid, low = halves(lo)
    out = None
    for f in range(face_count):
        pick = jnp.where(same & (code == f * elem_count + row_e), 1.0, 0.0).astype(bf16)
        cut = slice(f * width, (f + 1) * width)
        stack = jnp.concatenate([hi[cut], mid[cut], low[cut]], axis=0).astype(bf16)
        got = mm(stack, pick)
        got = got[:width] + got[width : 2 * width] + got[2 * width :]
        out = got if out is None else out + got
    out_ref[...] = out


def first_kernel(dofs_ref, stiff_ref, proj_ref, star_ref, send_ref,
                 first_ref, second_ref, faces_ref, bh_ref, bl_ref, x0_ref, out_ref):
    dims, var_count, _, elem_count = star_ref.shape
    face_count = proj_ref.shape[0]
    cols = var_count * elem_count
    x = jnp.concatenate([dofs_ref[v] for v in range(var_count)], axis=1)
    x0_ref[...] = x
    lane = lax.broadcasted_iota(jnp.int32, (elem_count, cols), 1) % elem_count
    keep = lane == lax.broadcasted_iota(jnp.int32, (elem_count, cols), 0)
    for d in range(dims):
        flat = jnp.concatenate([star_ref[d, v] for v in range(var_count)], axis=1)
        b = jnp.concatenate(
            [
                jnp.where(keep, jnp.broadcast_to(flat[w : w + 1], (elem_count, cols)), 0.0)
                for w in range(var_count)
            ],
            axis=0,
        )
        hi, lo = halves(b)
        bh_ref[d] = hi.astype(bf16)
        bl_ref[d] = lo.astype(bf16)
    form = left_form(stiff_rows(stiff_ref, False))
    first, second = series(
        form, x, bh_ref, bl_ref,
        [taylor_weights(0.0, fine_step, ORDER), taylor_weights(fine_step, 2.0 * fine_step, ORDER)],
    )
    first_ref[...] = first
    second_ref[...] = second
    faces_all = left(left_form(face_rows(proj_ref)), first)
    faces_ref[...] = faces_all
    export_rows(faces_all, send_ref, out_ref, var_count, elem_count, face_count)


def own_terms(base, x, faces_all, stiff_ref, proj_ref, bh_ref, bl_ref, ch_ref, cl_ref):
    face_count = proj_ref.shape[0]
    width = faces_all.shape[0] // face_count
    volume = star_apply(left_form(stiff_rows(stiff_ref, True)), x, bh_ref, bl_ref)
    wide = jnp.concatenate(
        [faces_all[f * width : (f + 1) * width] for f in range(face_count)], axis=1
    )
    flux = jnp.concatenate(
        [right(wide, ch_ref[f], cl_ref[f]) for f in range(face_count)], axis=0
    )
    return base + volume - left(left_form(face_rows(proj_ref).T), flux)


def own_first_kernel(x0_ref, first_ref, faces_ref, stiff_ref, proj_ref, bh_ref, bl_ref,
                     minus_ref, plus_ref, fault_flux_ref, fault_ref, source_ref, sub_ref,
                     acc_ref, ch_ref, cl_ref, rh_ref, rl_ref, *, sub_count, slots):
    face_count, var_count, _, elem_count = minus_ref.shape
    cols = var_count * elem_count
    lane = lax.broadcasted_iota(jnp.int32, (elem_count, cols), 1) % elem_count
    row = lax.broadcasted_iota(jnp.int32, (elem_count, cols), 0)
    keep = lane == row
    eye = (
        lax.broadcasted_iota(jnp.int32, (var_count, var_count), 0)
        == lax.broadcasted_iota(jnp.int32, (var_count, var_count), 1)
    )
    fault_flux = fault_flux_ref[...]
    columns = []
    for v in range(var_count):
        line = jnp.broadcast_to(fault_flux[v : v + 1], (var_count, var_count))
        column = jnp.sum(jnp.where(eye, line, 0.0), axis=1, keepdims=True)
        columns.append(jnp.broadcast_to(column, (var_count, elem_count)))
    friction = jnp.concatenate(columns, axis=1)
    own_sub = sub_ref[0]
    remote_rows = 3 * sub_count * var_count * slots
    group = var_count * slots
    rrow = lax.broadcasted_iota(jnp.int32, (group, cols), 0)
    rslot = rrow % slots
    for f in range(face_count):
        source = jnp.concatenate([source_ref[f : f + 1, :]] * var_count, axis=1)
        fault = jnp.concatenate([fault_ref[f : f + 1, :]] * var_count, axis=1)
        plus = jnp.concatenate([plus_ref[f, v] for v in range(var_count)], axis=1)
        minus = jnp.concatenate([minus_ref[f, v] for v in range(var_count)], axis=1)
        couple = jnp.where(fault == 1, friction, plus)
        for g in range(face_count):
            match = (source - g * elem_count) == row
            blocks = []
            for w in range(var_count):
                block = jnp.where(match, couple[w : w + 1], 0.0)
                if g == f:
                    block = block + jnp.where(keep, minus[w : w + 1], 0.0)
                blocks.append(block)
            hi, lo = halves(jnp.concatenate(blocks, axis=0))
            ch_ref[f, g * cols : (g + 1) * cols] = hi.astype(bf16)
            cl_ref[f, g * cols : (g + 1) * cols] = lo.astype(bf16)
        grown = jnp.concatenate(
            [jnp.broadcast_to(couple[w : w + 1], (slots, cols)) for w in range(var_count)], axis=0
        )
        pieces = []
        for side in range(3):
            for delta in range(sub_count):
                place = (own_sub + delta) % sub_count
                start = face_count * elem_count + (side * sub_count + place) * slots
                pieces.append(jnp.where((source - start) == rslot, grown, 0.0))
        hi, lo = halves(jnp.concatenate(pieces, axis=0))
        rh_ref[f] = hi.astype(bf16)
        rl_ref[f] = lo.astype(bf16)
    acc_ref[...] = own_terms(x0_ref[...], first_ref[...], faces_ref[...], stiff_ref, proj_ref,
                             bh_ref, bl_ref, ch_ref, cl_ref)


def remote_terms(acc_ref, message_refs, rh_ref, rl_ref, proj_ref):
    wide = jnp.concatenate([m[...] for m in message_refs], axis=1)
    flux = jnp.concatenate(
        [right(wide, rh_ref[f], rl_ref[f]) for f in range(rh_ref.shape[0])], axis=0
    )
    return acc_ref[...] - left(left_form(face_rows(proj_ref).T), flux)


def middle_kernel(acc_ref, rh_ref, rl_ref, stiff_ref, proj_ref, bh_ref, bl_ref, second_ref,
                  levels_ref, send_ref, *rest):
    message_refs, (moved_ref, carried_ref, faces_ref, out_ref) = rest[:-4], rest[-4:]
    elem_count = levels_ref.shape[1]
    var_count = acc_ref.shape[1] // elem_count
    moved = remote_terms(acc_ref, message_refs, rh_ref, rl_ref, proj_ref)
    moved_ref[...] = moved
    form = left_form(stiff_rows(stiff_ref, False))
    (fine,) = series(form, moved, bh_ref, bl_ref, [taylor_weights(0.0, fine_step, ORDER)])
    levels = jnp.concatenate([levels_ref[...]] * var_count, axis=1)
    carried = jnp.where(levels == 0, fine, second_ref[...])
    carried_ref[...] = carried
    faces_all = left(left_form(face_rows(proj_ref)), carried)
    faces_ref[...] = faces_all
    export_rows(faces_all, send_ref, out_ref, var_count, elem_count, proj_ref.shape[0])


def own_second_kernel(moved_ref, carried_ref, faces_ref, stiff_ref, proj_ref, bh_ref, bl_ref,
                      ch_ref, cl_ref, acc_ref):
    acc_ref[...] = own_terms(moved_ref[...], carried_ref[...], faces_ref[...], stiff_ref, proj_ref,
                             bh_ref, bl_ref, ch_ref, cl_ref)


def last_kernel(acc_ref, rh_ref, rl_ref, proj_ref, *rest):
    message_refs, out_ref = rest[:-1], rest[-1]
    out = remote_terms(acc_ref, message_refs, rh_ref, rl_ref, proj_ref)
    var_count, _, elem_count = out_ref.shape
    for v in range(var_count):
        out_ref[v] = out[:, v * elem_count : (v + 1) * elem_count]


def exchange(message):
    dom_count, sub_count = lax.axis_size("dom"), lax.axis_size("sub")
    got = []
    for side in range(3):
        for delta in range(sub_count):
            if side == 1 and delta == 0:
                got.append(message)
                continue
            pairs = []
            for dom in range(dom_count):
                for sub in range(sub_count):
                    origin = ((dom + side - 1) % dom_count) * sub_count + (sub + delta) % sub_count
                    pairs.append((origin, dom * sub_count + sub))
            got.append(lax.ppermute(message, ("dom", "sub"), pairs))
    return got


def call(kernel, places, shapes, *operands, cost=None):
    spec = {"v": pl.BlockSpec(memory_space=pltpu.VMEM), "s": pl.BlockSpec(memory_space=pltpu.SMEM)}
    outs = [jax.ShapeDtypeStruct(s, t) for s, t in shapes]
    single = len(outs) == 1
    return pl.pallas_call(
        kernel,
        in_specs=[spec[p] for p in places],
        out_specs=spec["v"] if single else [spec["v"]] * len(outs),
        out_shape=outs[0] if single else outs,
        cost_estimate=cost,
    )(*operands)


def per_device(
    dofs,
    stiffness,
    projection,
    star,
    flux_minus,
    flux_plus,
    fault_flux,
    fault_faces,
    levels,
    face_source,
    send_source,
):
    var_count, modes, elem_count = dofs.shape
    face_count, face_modes, _ = projection.shape
    dims = stiffness.shape[0]
    slots = send_source.shape[0]
    sub_count = lax.axis_size("sub")
    cols = var_count * elem_count
    width = face_pad(face_modes)
    field = ((modes, cols), f32)
    faces_shape = ((face_count * width, cols), f32)
    block = ((dims, cols, cols), bf16)
    sent = ((width, var_count * slots), f32)
    local = ((face_count, face_count * cols, cols), bf16)
    remote = ((face_count, 3 * sub_count * var_count * slots, cols), bf16)
    sub_index = lax.axis_index("sub").reshape(1).astype(jnp.int32)
    levels_row = levels.reshape(1, elem_count)
    work = pl.CostEstimate(flops=400_000_000, bytes_accessed=4_000_000, transcendentals=0)

    first, second, faces_first, bh, bl, x0, message = call(
        first_kernel, "vvvvs", [field, field, faces_shape, block, block, field, sent],
        dofs, stiffness, projection, star, send_source,
    )
    got = exchange(message)
    acc, ch, cl, rh, rl = call(
        lambda *refs: own_first_kernel(*refs, sub_count=sub_count, slots=slots),
        "v" * 12 + "s", [field, local, local, remote, remote],
        x0, first, faces_first, stiffness, projection, bh, bl, flux_minus, flux_plus,
        fault_flux, fault_faces, face_source, sub_index, cost=work,
    )
    count = len(got)
    moved, carried, faces_carried, message = call(
        middle_kernel, "v" * 9 + "s" + "v" * count, [field, field, faces_shape, sent],
        acc, rh, rl, stiffness, projection, bh, bl, second, levels_row, send_source, *got,
    )
    got = exchange(message)
    acc = call(
        own_second_kernel, "v" * 9, [field],
        moved, carried, faces_carried, stiffness, projection, bh, bl, ch, cl, cost=work,
    )
    return call(
        last_kernel, "v" * 4 + "v" * count, [(dofs.shape, f32)],
        acc, rh, rl, projection, *got,
    )


def solution(mesh):
    return jax.shard_map(
        per_device,
        mesh=mesh,
        in_specs=(
            P(None, None, ("dom", "sub")),
            P(),
            P(),
            P(None, None, None, ("dom", "sub")),
            P(None, None, None, ("dom", "sub")),
            P(None, None, None, ("dom", "sub")),
            P(),
            P(None, ("dom", "sub")),
            P(("dom", "sub")),
            P(None, ("dom", "sub")),
            P(("dom", "sub")),
        ),
        out_specs=P(None, None, ("dom", "sub")),
        check_vma=False,
    )
```

```python
import math

import jax
import jax.numpy as jnp
from jax import lax
from jax.experimental import pallas as pl
from jax.experimental.pallas import tpu as pltpu
from jax.sharding import PartitionSpec as P

ORDER = 6

fine_step = 0.75
f32 = jnp.float32
bf16 = jnp.bfloat16


def taylor_weights(start_time, stop_time, term_count):
    return [
        (stop_time ** (term + 1) - start_time ** (term + 1)) / math.factorial(term + 1)
        for term in range(term_count)
    ]


def mm(a, b):
    return jnp.dot(a, b, preferred_element_type=f32)


def halves(x):
    hi = x.astype(bf16).astype(f32)
    return hi, x - hi


def left_form(a):
    hi, lo = halves(a)
    return jnp.concatenate([hi, hi, lo], axis=1).astype(bf16)


def left(form, x):
    hi, lo = halves(x)
    return mm(form, jnp.concatenate([hi, lo, hi], axis=0).astype(bf16))


def right(x, b_hi, b_lo):
    rows = x.shape[0]
    hi, lo = halves(x)
    both = mm(jnp.concatenate([hi, lo], axis=0).astype(bf16), b_hi)
    return both[:rows] + both[rows:] + mm(hi.astype(bf16), b_lo)


def stiff_rows(stiff_ref, flip):
    mats = [stiff_ref[d] for d in range(stiff_ref.shape[0])]
    return jnp.concatenate([m.T if flip else m for m in mats], axis=0)


def face_pad(face_modes):
    return -(-face_modes // 8) * 8


def face_rows(proj_ref):
    width, faces, modes = proj_ref.shape
    gap = face_pad(width) - width
    parts = []
    for f in range(faces):
        block = proj_ref[:, f, :]
        if gap:
            block = jnp.concatenate([block, jnp.zeros((gap, modes), f32)], axis=0)
        parts.append(block)
    return jnp.concatenate(parts, axis=0)


def star_apply(form, x, bh_ref, bl_ref):
    t = left(form, x)
    rows = x.shape[0]
    out = None
    for d in range(bh_ref.shape[0]):
        term = right(t[d * rows : (d + 1) * rows], bh_ref[d], bl_ref[d])
        out = term if out is None else out + term
    return out


def series(form, x, bh_ref, bl_ref, weight_lists):
    sums = [x * f32(ws[0]) for ws in weight_lists]
    for k in range(1, ORDER):
        x = star_apply(form, x, bh_ref, bl_ref)
        sums = [s + x * f32(ws[k]) for s, ws in zip(sums, weight_lists)]
    return sums


def export_rows(faces_all, send_ref, out_ref, var_count, elem_count, face_count):
    slots = send_ref.shape[0]
    cols = var_count * slots
    rows = var_count * elem_count
    width = faces_all.shape[0] // face_count
    row = lax.broadcasted_iota(jnp.int32, (rows, cols), 0)
    col = lax.broadcasted_iota(jnp.int32, (rows, cols), 1)
    row_v, row_e = row // elem_count, row % elem_count
    col_v, col_s = col // slots, col % slots
    code = jnp.zeros((rows, cols), jnp.int32)
    for s in range(slots):
        code = jnp.where(col_s == s, send_ref[s], code)
    same = row_v == col_v
    hi, lo = halves(faces_all)
    mid, low = halves(lo)
    out = None
    for f in range(face_count):
        pick = jnp.where(same & (code == f * elem_count + row_e), 1.0, 0.0).astype(bf16)
        cut = slice(f * width, (f + 1) * width)
        stack = jnp.concatenate([hi[cut], mid[cut], low[cut]], axis=0).astype(bf16)
        got = mm(stack, pick)
        got = got[:width] + got[width : 2 * width] + got[2 * width :]
        out = got if out is None else out + got
    out_ref[...] = out


def first_kernel(dofs_ref, stiff_ref, proj_ref, star_ref, send_ref,
                 first_ref, second_ref, faces_ref, bh_ref, bl_ref, x0_ref, out_ref, rows_ref):
    var_count, _, dims, elem_count = star_ref.shape
    face_count = proj_ref.shape[1]
    cols = var_count * elem_count
    x = dofs_ref[...].T
    x0_ref[...] = x
    lane = lax.broadcasted_iota(jnp.int32, (elem_count, cols), 1) % elem_count
    keep = lane == lax.broadcasted_iota(jnp.int32, (elem_count, cols), 0)
    flats = [
        jnp.concatenate([star_ref[v, w] for v in range(var_count)], axis=1)
        for w in range(var_count)
    ]
    for d in range(dims):
        b = jnp.concatenate(
            [
                jnp.where(keep, jnp.broadcast_to(flats[w][d : d + 1], (elem_count, cols)), 0.0)
                for w in range(var_count)
            ],
            axis=0,
        )
        hi, lo = halves(b)
        bh_ref[d] = hi.astype(bf16)
        bl_ref[d] = lo.astype(bf16)
    form = left_form(stiff_rows(stiff_ref, False))
    first, second = series(
        form, x, bh_ref, bl_ref,
        [taylor_weights(0.0, fine_step, ORDER), taylor_weights(fine_step, 2.0 * fine_step, ORDER)],
    )
    first_ref[...] = first
    second_ref[...] = second
    rows_all = face_rows(proj_ref)
    rows_ref[...] = rows_all
    faces_all = left(left_form(rows_all), first)
    faces_ref[...] = faces_all
    export_rows(faces_all, send_ref, out_ref, var_count, elem_count, face_count)


def own_terms(base, x, faces_all, stiff_ref, rows_ref, bh_ref, bl_ref, ch_ref, cl_ref):
    face_count = ch_ref.shape[0]
    width = faces_all.shape[0] // face_count
    volume = star_apply(left_form(stiff_rows(stiff_ref, True)), x, bh_ref, bl_ref)
    wide = jnp.concatenate(
        [faces_all[f * width : (f + 1) * width] for f in range(face_count)], axis=1
    )
    flux = jnp.concatenate(
        [right(wide, ch_ref[f], cl_ref[f]) for f in range(face_count)], axis=0
    )
    return base + volume - left(left_form(rows_ref[...].T), flux)


def matrices_kernel(minus_ref, plus_ref, fault_flux_ref, fault_ref, source_ref, sub_ref,
                    ch_ref, cl_ref, rh_ref, rl_ref, *, sub_count, slots):
    var_count, _, face_count, elem_count = minus_ref.shape
    cols = var_count * elem_count
    lane = lax.broadcasted_iota(jnp.int32, (elem_count, cols), 1) % elem_count
    row = lax.broadcasted_iota(jnp.int32, (elem_count, cols), 0)
    keep = lane == row
    eye = (
        lax.broadcasted_iota(jnp.int32, (var_count, var_count), 0)
        == lax.broadcasted_iota(jnp.int32, (var_count, var_count), 1)
    )
    fault_flux = fault_flux_ref[...]
    columns = []
    for v in range(var_count):
        line = jnp.broadcast_to(fault_flux[v : v + 1], (var_count, var_count))
        column = jnp.sum(jnp.where(eye, line, 0.0), axis=1, keepdims=True)
        columns.append(jnp.broadcast_to(column, (var_count, elem_count)))
    friction = jnp.concatenate(columns, axis=1)
    own_sub = sub_ref[0]
    group = var_count * slots
    rslot = lax.broadcasted_iota(jnp.int32, (group, cols), 0) % slots
    sources = jnp.concatenate([source_ref[...]] * var_count, axis=1)
    faults = jnp.concatenate([fault_ref[...]] * var_count, axis=1)
    couples, minuses = [], []
    for w in range(var_count):
        plus = jnp.concatenate([plus_ref[v, w] for v in range(var_count)], axis=1)
        minuses.append(jnp.concatenate([minus_ref[v, w] for v in range(var_count)], axis=1))
        couples.append(jnp.where(faults == 1, friction[w : w + 1], plus))
    for f in range(face_count):
        source = sources[f : f + 1]
        for g in range(face_count):
            match = (source - g * elem_count) == row
            blocks = []
            for w in range(var_count):
                block = jnp.where(match, couples[w][f : f + 1], 0.0)
                if g == f:
                    block = block + jnp.where(keep, minuses[w][f : f + 1], 0.0)
                blocks.append(block)
            hi, lo = halves(jnp.concatenate(blocks, axis=0))
            ch_ref[f, g * cols : (g + 1) * cols] = hi.astype(bf16)
            cl_ref[f, g * cols : (g + 1) * cols] = lo.astype(bf16)
        grown = jnp.concatenate(
            [jnp.broadcast_to(c[f : f + 1], (slots, cols)) for c in couples], axis=0
        )
        pieces = []
        for side in range(3):
            for delta in range(sub_count):
                place = (own_sub + delta) % sub_count
                start = face_count * elem_count + (side * sub_count + place) * slots
                pieces.append(jnp.where((source - start) == rslot, grown, 0.0))
        hi, lo = halves(jnp.concatenate(pieces, axis=0))
        rh_ref[f] = hi.astype(bf16)
        rl_ref[f] = lo.astype(bf16)


def remote_terms(acc_ref, message_refs, rh_ref, rl_ref, rows_ref):
    width = rows_ref.shape[0] // rh_ref.shape[0]
    wide = jnp.concatenate(
        [m[k : k + width] for m in message_refs for k in range(0, m.shape[0], width)], axis=1
    )
    flux = jnp.concatenate(
        [right(wide, rh_ref[f], rl_ref[f]) for f in range(rh_ref.shape[0])], axis=0
    )
    return acc_ref[...] - left(left_form(rows_ref[...].T), flux)


def middle_kernel(acc_ref, rh_ref, rl_ref, stiff_ref, rows_ref, bh_ref, bl_ref, second_ref,
                  levels_ref, send_ref, *rest):
    message_refs, (moved_ref, carried_ref, faces_ref, out_ref) = rest[:-4], rest[-4:]
    elem_count = levels_ref.shape[1]
    var_count = acc_ref.shape[1] // elem_count
    moved = remote_terms(acc_ref, message_refs, rh_ref, rl_ref, rows_ref)
    moved_ref[...] = moved
    form = left_form(stiff_rows(stiff_ref, False))
    (fine,) = series(form, moved, bh_ref, bl_ref, [taylor_weights(0.0, fine_step, ORDER)])
    levels = jnp.concatenate([levels_ref[...]] * var_count, axis=1)
    carried = jnp.where(levels == 0, fine, second_ref[...])
    carried_ref[...] = carried
    faces_all = left(left_form(rows_ref[...]), carried)
    faces_ref[...] = faces_all
    export_rows(faces_all, send_ref, out_ref, var_count, elem_count, rh_ref.shape[0])


def own_kernel(base_ref, x_ref, faces_ref, stiff_ref, rows_ref, bh_ref, bl_ref,
               ch_ref, cl_ref, acc_ref):
    acc_ref[...] = own_terms(base_ref[...], x_ref[...], faces_ref[...], stiff_ref, rows_ref,
                             bh_ref, bl_ref, ch_ref, cl_ref)


def last_kernel(acc_ref, rh_ref, rl_ref, rows_ref, *rest):
    message_refs, out_ref = rest[:-1], rest[-1]
    out_ref[...] = remote_terms(acc_ref, message_refs, rh_ref, rl_ref, rows_ref).T


def exchange(message):
    dom_count, sub_count = lax.axis_size("dom"), lax.axis_size("sub")
    group = [message]
    for delta in range(1, sub_count):
        pairs = [((sub + delta) % sub_count, sub) for sub in range(sub_count)]
        group.append(lax.ppermute(message, "sub", pairs))
    group = jnp.concatenate(group, axis=0)
    up = [(i, (i + 1) % dom_count) for i in range(dom_count)]
    down = [(j, i) for i, j in up]
    return [lax.ppermute(group, "dom", up), group, lax.ppermute(group, "dom", down)]


def call(kernel, places, shapes, *operands, cost=None):
    spec = {"v": pl.BlockSpec(memory_space=pltpu.VMEM), "s": pl.BlockSpec(memory_space=pltpu.SMEM)}
    outs = [jax.ShapeDtypeStruct(s, t) for s, t in shapes]
    single = len(outs) == 1
    return pl.pallas_call(
        kernel,
        in_specs=[spec[p] for p in places],
        out_specs=spec["v"] if single else [spec["v"]] * len(outs),
        out_shape=outs[0] if single else outs,
        cost_estimate=cost,
    )(*operands)


def per_device(
    dofs,
    stiffness,
    projection,
    star,
    flux_minus,
    flux_plus,
    fault_flux,
    fault_faces,
    levels,
    face_source,
    send_source,
):
    var_count, modes, elem_count = dofs.shape
    face_count, face_modes, _ = projection.shape
    dims = stiffness.shape[0]
    slots = send_source.shape[0]
    sub_count = lax.axis_size("sub")
    cols = var_count * elem_count
    width = face_pad(face_modes)
    field = ((modes, cols), f32)
    faces_shape = ((face_count * width, cols), f32)
    block = ((dims, cols, cols), bf16)
    sent = ((width, var_count * slots), f32)
    local = ((face_count, face_count * cols, cols), bf16)
    remote = ((face_count, 3 * sub_count * var_count * slots, cols), bf16)
    sub_index = lax.axis_index("sub").reshape(1).astype(jnp.int32)
    levels_row = levels.reshape(1, elem_count)
    work = pl.CostEstimate(flops=400_000_000, bytes_accessed=4_000_000, transcendentals=0)

    dofs_view = jnp.transpose(dofs, (0, 2, 1)).reshape(cols, modes)
    star_view = jnp.transpose(star, (1, 2, 0, 3))
    minus_view = jnp.transpose(flux_minus, (1, 2, 0, 3))
    plus_view = jnp.transpose(flux_plus, (1, 2, 0, 3))
    projection_view = jnp.transpose(projection, (1, 0, 2))
    first, second, faces_first, bh, bl, x0, message, rows = call(
        first_kernel, "vvvvs",
        [field, field, faces_shape, block, block, field, sent, ((face_count * width, modes), f32)],
        dofs_view, stiffness, projection_view, star_view, send_source,
    )
    got = exchange(message)
    ch, cl, rh, rl = call(
        lambda *refs: matrices_kernel(*refs, sub_count=sub_count, slots=slots),
        "v" * 5 + "s", [local, local, remote, remote],
        minus_view, plus_view, fault_flux, fault_faces, face_source, sub_index, cost=work,
    )
    acc = call(
        own_kernel, "v" * 9, [field],
        x0, first, faces_first, stiffness, rows, bh, bl, ch, cl, cost=work,
    )
    count = len(got)
    moved, carried, faces_carried, message = call(
        middle_kernel, "v" * 9 + "s" + "v" * count, [field, field, faces_shape, sent],
        acc, rh, rl, stiffness, rows, bh, bl, second, levels_row, send_source, *got,
    )
    got = exchange(message)
    acc = call(
        own_kernel, "v" * 9, [field],
        moved, carried, faces_carried, stiffness, rows, bh, bl, ch, cl, cost=work,
    )
    out = call(
        last_kernel, "v" * 4 + "v" * count, [((cols, modes), f32)],
        acc, rh, rl, rows, *got,
    )
    return jnp.transpose(out.reshape(var_count, elem_count, modes), (0, 2, 1))


def solution(mesh):
    return jax.shard_map(
        per_device,
        mesh=mesh,
        in_specs=(
            P(None, None, ("dom", "sub")),
            P(),
            P(),
            P(None, None, None, ("dom", "sub")),
            P(None, None, None, ("dom", "sub")),
            P(None, None, None, ("dom", "sub")),
            P(),
            P(None, ("dom", "sub")),
            P(("dom", "sub")),
            P(None, ("dom", "sub")),
            P(("dom", "sub")),
        ),
        out_specs=P(None, None, ("dom", "sub")),
        check_vma=False,
    )
```

```python
import math

import jax
import jax.numpy as jnp
from jax import lax
from jax.experimental import pallas as pl
from jax.experimental.pallas import tpu as pltpu
from jax.sharding import PartitionSpec as P

ORDER = 6

fine_step = 0.75
f32 = jnp.float32
bf16 = jnp.bfloat16


def taylor_weights(start_time, stop_time, term_count):
    return [
        (stop_time ** (term + 1) - start_time ** (term + 1)) / math.factorial(term + 1)
        for term in range(term_count)
    ]


def mm(a, b):
    return jnp.dot(a, b, preferred_element_type=f32)


def halves(x):
    hi = x.astype(bf16).astype(f32)
    return hi, x - hi


def left_form(a):
    hi, lo = halves(a)
    return jnp.concatenate([hi, hi, lo], axis=1).astype(bf16)


def left(form, x):
    hi, lo = halves(x)
    return mm(form, jnp.concatenate([hi, lo, hi], axis=0).astype(bf16))


def right(x, b_hi, b_lo):
    rows = x.shape[0]
    hi, lo = halves(x)
    both = mm(jnp.concatenate([hi, lo], axis=0).astype(bf16), b_hi)
    return both[:rows] + both[rows:] + mm(hi.astype(bf16), b_lo)


def stiff_rows(stiff_ref, flip):
    mats = [stiff_ref[d] for d in range(stiff_ref.shape[0])]
    return jnp.concatenate([m.T if flip else m for m in mats], axis=0)


def face_pad(face_modes):
    return -(-face_modes // 8) * 8


def face_rows(proj_ref):
    width, faces, modes = proj_ref.shape
    gap = face_pad(width) - width
    parts = []
    for f in range(faces):
        block = proj_ref[:, f, :]
        if gap:
            block = jnp.concatenate([block, jnp.zeros((gap, modes), f32)], axis=0)
        parts.append(block)
    return jnp.concatenate(parts, axis=0)


def star_apply(form, x, bh_ref, bl_ref):
    t = left(form, x)
    rows = x.shape[0]
    out = None
    for d in range(bh_ref.shape[0]):
        term = right(t[d * rows : (d + 1) * rows], bh_ref[d], bl_ref[d])
        out = term if out is None else out + term
    return out


def series(form, x, bh_ref, bl_ref, weight_lists):
    sums = [x * f32(ws[0]) for ws in weight_lists]
    for k in range(1, ORDER):
        x = star_apply(form, x, bh_ref, bl_ref)
        sums = [s + x * f32(ws[k]) for s, ws in zip(sums, weight_lists)]
    return sums


def export_rows(faces_all, send_ref, out_ref, var_count, elem_count, face_count):
    slots = send_ref.shape[0]
    cols = var_count * slots
    rows = var_count * elem_count
    width = faces_all.shape[0] // face_count
    row = lax.broadcasted_iota(jnp.int32, (rows, cols), 0)
    col = lax.broadcasted_iota(jnp.int32, (rows, cols), 1)
    row_v, row_e = row // elem_count, row % elem_count
    col_v, col_s = col // slots, col % slots
    code = jnp.zeros((rows, cols), jnp.int32)
    for s in range(slots):
        code = jnp.where(col_s == s, send_ref[s], code)
    same = row_v == col_v
    hi, lo = halves(faces_all)
    mid, low = halves(lo)
    out = None
    for f in range(face_count):
        pick = jnp.where(same & (code == f * elem_count + row_e), 1.0, 0.0).astype(bf16)
        cut = slice(f * width, (f + 1) * width)
        stack = jnp.concatenate([hi[cut], mid[cut], low[cut]], axis=0).astype(bf16)
        got = mm(stack, pick)
        got = got[:width] + got[width : 2 * width] + got[2 * width :]
        out = got if out is None else out + got
    out_ref[...] = out


def first_kernel(dofs_ref, stiff_ref, proj_ref, star_ref, send_ref,
                 first_ref, second_ref, faces_ref, bh_ref, bl_ref, x0_ref, out_ref, rows_ref):
    var_count, _, dims, elem_count = star_ref.shape
    face_count = proj_ref.shape[1]
    cols = var_count * elem_count
    x = dofs_ref[...].T
    x0_ref[...] = x
    lane = lax.broadcasted_iota(jnp.int32, (elem_count, cols), 1) % elem_count
    keep = lane == lax.broadcasted_iota(jnp.int32, (elem_count, cols), 0)
    flats = [
        jnp.concatenate([star_ref[v, w] for v in range(var_count)], axis=1)
        for w in range(var_count)
    ]
    for d in range(dims):
        b = jnp.concatenate(
            [
                jnp.where(keep, jnp.broadcast_to(flats[w][d : d + 1], (elem_count, cols)), 0.0)
                for w in range(var_count)
            ],
            axis=0,
        )
        hi, lo = halves(b)
        bh_ref[d] = hi.astype(bf16)
        bl_ref[d] = lo.astype(bf16)
    form = left_form(stiff_rows(stiff_ref, False))
    first, second = series(
        form, x, bh_ref, bl_ref,
        [taylor_weights(0.0, fine_step, ORDER), taylor_weights(fine_step, 2.0 * fine_step, ORDER)],
    )
    first_ref[...] = first
    second_ref[...] = second
    rows_all = face_rows(proj_ref)
    rows_ref[...] = rows_all
    faces_all = left(left_form(rows_all), first)
    faces_ref[...] = faces_all
    export_rows(faces_all, send_ref, out_ref, var_count, elem_count, face_count)


def own_terms(base, x, faces_all, stiff_ref, rows_ref, bh_ref, bl_ref, ch_ref, cl_ref):
    face_count = ch_ref.shape[0]
    width = faces_all.shape[0] // face_count
    volume = star_apply(left_form(stiff_rows(stiff_ref, True)), x, bh_ref, bl_ref)
    wide = jnp.concatenate(
        [faces_all[f * width : (f + 1) * width] for f in range(face_count)], axis=1
    )
    flux = jnp.concatenate(
        [right(wide, ch_ref[f], cl_ref[f]) for f in range(face_count)], axis=0
    )
    return base + volume - left(left_form(rows_ref[...].T), flux)


def matrices_kernel(minus_ref, plus_ref, fault_flux_ref, fault_ref, source_ref, sub_ref,
                    ch_ref, cl_ref, rh_ref, rl_ref, *, sub_count, slots):
    var_count, _, face_count, elem_count = minus_ref.shape
    cols = var_count * elem_count
    lane = lax.broadcasted_iota(jnp.int32, (elem_count, cols), 1) % elem_count
    row = lax.broadcasted_iota(jnp.int32, (elem_count, cols), 0)
    keep = lane == row
    eye = (
        lax.broadcasted_iota(jnp.int32, (var_count, var_count), 0)
        == lax.broadcasted_iota(jnp.int32, (var_count, var_count), 1)
    )
    fault_flux = fault_flux_ref[...]
    columns = []
    for v in range(var_count):
        line = jnp.broadcast_to(fault_flux[v : v + 1], (var_count, var_count))
        column = jnp.sum(jnp.where(eye, line, 0.0), axis=1, keepdims=True)
        columns.append(jnp.broadcast_to(column, (var_count, elem_count)))
    friction = jnp.concatenate(columns, axis=1)
    own_sub = sub_ref[0]
    group = var_count * slots
    rslot = lax.broadcasted_iota(jnp.int32, (group, cols), 0) % slots
    sources = jnp.concatenate([source_ref[...]] * var_count, axis=1)
    faults = jnp.concatenate([fault_ref[...]] * var_count, axis=1)
    couples, minuses = [], []
    for w in range(var_count):
        plus = jnp.concatenate([plus_ref[v, w] for v in range(var_count)], axis=1)
        minuses.append(jnp.concatenate([minus_ref[v, w] for v in range(var_count)], axis=1))
        couples.append(jnp.where(faults == 1, friction[w : w + 1], plus))
    for f in range(face_count):
        source = sources[f : f + 1]
        for g in range(face_count):
            match = (source - g * elem_count) == row
            blocks = []
            for w in range(var_count):
                block = jnp.where(match, couples[w][f : f + 1], 0.0)
                if g == f:
                    block = block + jnp.where(keep, minuses[w][f : f + 1], 0.0)
                blocks.append(block)
            hi, lo = halves(jnp.concatenate(blocks, axis=0))
            ch_ref[f, g * cols : (g + 1) * cols] = hi.astype(bf16)
            cl_ref[f, g * cols : (g + 1) * cols] = lo.astype(bf16)
        grown = jnp.concatenate(
            [jnp.broadcast_to(c[f : f + 1], (slots, cols)) for c in couples], axis=0
        )
        pieces = []
        for side in range(3):
            for delta in range(sub_count):
                place = (own_sub + delta) % sub_count
                start = face_count * elem_count + (side * sub_count + place) * slots
                pieces.append(jnp.where((source - start) == rslot, grown, 0.0))
        hi, lo = halves(jnp.concatenate(pieces, axis=0))
        rh_ref[f] = hi.astype(bf16)
        rl_ref[f] = lo.astype(bf16)


def remote_terms(acc_ref, message_refs, rh_ref, rl_ref, rows_ref):
    width = rows_ref.shape[0] // rh_ref.shape[0]
    wide = jnp.concatenate(
        [m[k : k + width] for m in message_refs for k in range(0, m.shape[0], width)], axis=1
    )
    flux = jnp.concatenate(
        [right(wide, rh_ref[f], rl_ref[f]) for f in range(rh_ref.shape[0])], axis=0
    )
    return acc_ref[...] - left(left_form(rows_ref[...].T), flux)


def middle_kernel(acc_ref, rh_ref, rl_ref, stiff_ref, rows_ref, bh_ref, bl_ref, second_ref,
                  levels_ref, send_ref, *rest):
    message_refs, (moved_ref, carried_ref, faces_ref, out_ref) = rest[:-4], rest[-4:]
    elem_count = levels_ref.shape[1]
    var_count = acc_ref.shape[1] // elem_count
    moved = remote_terms(acc_ref, message_refs, rh_ref, rl_ref, rows_ref)
    moved_ref[...] = moved
    form = left_form(stiff_rows(stiff_ref, False))
    (fine,) = series(form, moved, bh_ref, bl_ref, [taylor_weights(0.0, fine_step, ORDER)])
    levels = jnp.concatenate([levels_ref[...]] * var_count, axis=1)
    carried = jnp.where(levels == 0, fine, second_ref[...])
    carried_ref[...] = carried
    faces_all = left(left_form(rows_ref[...]), carried)
    faces_ref[...] = faces_all
    export_rows(faces_all, send_ref, out_ref, var_count, elem_count, rh_ref.shape[0])


def own_kernel(base_ref, x_ref, faces_ref, stiff_ref, rows_ref, bh_ref, bl_ref,
               ch_ref, cl_ref, acc_ref):
    acc_ref[...] = own_terms(base_ref[...], x_ref[...], faces_ref[...], stiff_ref, rows_ref,
                             bh_ref, bl_ref, ch_ref, cl_ref)


def last_kernel(acc_ref, rh_ref, rl_ref, rows_ref, *rest):
    message_refs, out_ref = rest[:-1], rest[-1]
    out_ref[...] = remote_terms(acc_ref, message_refs, rh_ref, rl_ref, rows_ref).T


def exchange(message):
    dom_count, sub_count = lax.axis_size("dom"), lax.axis_size("sub")
    group = [message]
    for delta in range(1, sub_count):
        pairs = [((sub + delta) % sub_count, sub) for sub in range(sub_count)]
        group.append(lax.ppermute(message, "sub", pairs))
    group = jnp.concatenate(group, axis=0)
    up = [(i, (i + 1) % dom_count) for i in range(dom_count)]
    down = [(j, i) for i, j in up]
    return [lax.ppermute(group, "dom", up), group, lax.ppermute(group, "dom", down)]


def pin(x):
    return pltpu.with_memory_space_constraint(x, pltpu.VMEM)


def call(kernel, places, shapes, *operands, cost=None):
    vmem = pl.BlockSpec(memory_space=pltpu.VMEM)
    spec = {"p": vmem, "v": vmem, "s": pl.BlockSpec(memory_space=pltpu.SMEM)}
    outs = [
        pltpu.VMEM(shape[0], shape[1]) if len(shape) > 2 else jax.ShapeDtypeStruct(*shape)
        for shape in shapes
    ]
    single = len(outs) == 1
    return pl.pallas_call(
        kernel,
        in_specs=[spec[p] for p in places],
        out_specs=vmem if single else [vmem] * len(outs),
        out_shape=outs[0] if single else outs,
        cost_estimate=cost,
    )(*[pin(x) if p == "p" else x for p, x in zip(places, operands)])


def per_device(
    dofs,
    stiffness,
    projection,
    star,
    flux_minus,
    flux_plus,
    fault_flux,
    fault_faces,
    levels,
    face_source,
    send_source,
):
    var_count, modes, elem_count = dofs.shape
    face_count, face_modes, _ = projection.shape
    dims = stiffness.shape[0]
    slots = send_source.shape[0]
    sub_count = lax.axis_size("sub")
    cols = var_count * elem_count
    width = face_pad(face_modes)
    field = ((modes, cols), f32, True)
    faces_shape = ((face_count * width, cols), f32, True)
    block = ((dims, cols, cols), bf16, True)
    sent = ((width, var_count * slots), f32, True)
    local = ((face_count, face_count * cols, cols), bf16)
    remote = ((face_count, 3 * sub_count * var_count * slots, cols), bf16)
    sub_index = lax.axis_index("sub").reshape(1).astype(jnp.int32)
    levels_row = levels.reshape(1, elem_count)
    work = pl.CostEstimate(flops=400_000_000, bytes_accessed=4_000_000, transcendentals=0)

    dofs_view = jnp.transpose(dofs, (0, 2, 1)).reshape(cols, modes)
    star_view = jnp.transpose(star, (1, 2, 0, 3))
    minus_view = jnp.transpose(flux_minus, (1, 2, 0, 3))
    plus_view = jnp.transpose(flux_plus, (1, 2, 0, 3))
    projection_view = jnp.transpose(projection, (1, 0, 2))
    first, second, faces_first, bh, bl, x0, message, rows = call(
        first_kernel, "vvvvs",
        [field, field, faces_shape, block, block, field, sent, ((face_count * width, modes), f32, True)],
        dofs_view, stiffness, projection_view, star_view, send_source,
    )
    got = exchange(message)
    ch, cl, rh, rl = call(
        lambda *refs: matrices_kernel(*refs, sub_count=sub_count, slots=slots),
        "v" * 5 + "s", [local, local, remote, remote],
        minus_view, plus_view, fault_flux, fault_faces, face_source, sub_index, cost=work,
    )
    acc = call(
        own_kernel, "pppvpppvv", [field],
        x0, first, faces_first, stiffness, rows, bh, bl, ch, cl, cost=work,
    )
    count = len(got)
    moved, carried, faces_carried, message = call(
        middle_kernel, "pvvvpppp" + "vs" + "p" * count, [field, field, faces_shape, sent],
        acc, rh, rl, stiffness, rows, bh, bl, second, levels_row, send_source, *got,
    )
    got = exchange(message)
    acc = call(
        own_kernel, "pppvpppvv", [field],
        moved, carried, faces_carried, stiffness, rows, bh, bl, ch, cl, cost=work,
    )
    out = call(
        last_kernel, "pvvp" + "p" * count, [((cols, modes), f32)],
        acc, rh, rl, rows, *got,
    )
    return jnp.transpose(out.reshape(var_count, elem_count, modes), (0, 2, 1))


def solution(mesh):
    return jax.shard_map(
        per_device,
        mesh=mesh,
        in_specs=(
            P(None, None, ("dom", "sub")),
            P(),
            P(),
            P(None, None, None, ("dom", "sub")),
            P(None, None, None, ("dom", "sub")),
            P(None, None, None, ("dom", "sub")),
            P(),
            P(None, ("dom", "sub")),
            P(("dom", "sub")),
            P(None, ("dom", "sub")),
            P(("dom", "sub")),
        ),
        out_specs=P(None, None, ("dom", "sub")),
        check_vma=False,
    )
```

```python
import math

import jax
import jax.numpy as jnp
from jax import lax
from jax.experimental import pallas as pl
from jax.experimental.pallas import tpu as pltpu
from jax.sharding import PartitionSpec as P

ORDER = 6

fine_step = 0.75
f32 = jnp.float32
bf16 = jnp.bfloat16


def taylor_weights(start_time, stop_time, term_count):
    return [
        (stop_time ** (term + 1) - start_time ** (term + 1)) / math.factorial(term + 1)
        for term in range(term_count)
    ]


def mm(a, b):
    return jnp.dot(a, b, preferred_element_type=f32)


def halves(x):
    hi = x.astype(bf16).astype(f32)
    return hi, x - hi


def left_form(a):
    hi, lo = halves(a)
    return jnp.concatenate([hi, hi, lo], axis=1).astype(bf16)


def left(form, x):
    hi, lo = halves(x)
    return mm(form, jnp.concatenate([hi, lo, hi], axis=0).astype(bf16))


def right(x, b_hi, b_lo):
    rows = x.shape[0]
    hi, lo = halves(x)
    both = mm(jnp.concatenate([hi, lo], axis=0).astype(bf16), b_hi)
    return both[:rows] + both[rows:] + mm(hi.astype(bf16), b_lo)


def stiff_rows(stiff_ref, flip):
    mats = [stiff_ref[d] for d in range(stiff_ref.shape[0])]
    return jnp.concatenate([m.T if flip else m for m in mats], axis=0)


def face_pad(face_modes):
    return -(-face_modes // 8) * 8


def face_rows(proj_ref):
    width, faces, modes = proj_ref.shape
    gap = face_pad(width) - width
    parts = []
    for f in range(faces):
        block = proj_ref[:, f, :]
        if gap:
            block = jnp.concatenate([block, jnp.zeros((gap, modes), f32)], axis=0)
        parts.append(block)
    return jnp.concatenate(parts, axis=0)


def star_apply(form, x, bh_ref, bl_ref):
    t = left(form, x)
    rows = x.shape[0]
    out = None
    for d in range(bh_ref.shape[0]):
        term = right(t[d * rows : (d + 1) * rows], bh_ref[d], bl_ref[d])
        out = term if out is None else out + term
    return out


def series(form, x, bh_ref, bl_ref, weight_lists):
    sums = [x * f32(ws[0]) for ws in weight_lists]
    for k in range(1, ORDER):
        x = star_apply(form, x, bh_ref, bl_ref)
        sums = [s + x * f32(ws[k]) for s, ws in zip(sums, weight_lists)]
    return sums


def export_rows(faces_all, send_ref, out_ref, var_count, elem_count, face_count):
    slots = send_ref.shape[0]
    cols = var_count * slots
    rows = var_count * elem_count
    width = faces_all.shape[0] // face_count
    row = lax.broadcasted_iota(jnp.int32, (rows, cols), 0)
    col = lax.broadcasted_iota(jnp.int32, (rows, cols), 1)
    row_v, row_e = row // elem_count, row % elem_count
    col_v, col_s = col // slots, col % slots
    code = jnp.zeros((rows, cols), jnp.int32)
    for s in range(slots):
        code = jnp.where(col_s == s, send_ref[s], code)
    same = row_v == col_v
    hi, lo = halves(faces_all)
    mid, low = halves(lo)
    out = None
    for f in range(face_count):
        pick = jnp.where(same & (code == f * elem_count + row_e), 1.0, 0.0).astype(bf16)
        cut = slice(f * width, (f + 1) * width)
        stack = jnp.concatenate([hi[cut], mid[cut], low[cut]], axis=0).astype(bf16)
        got = mm(stack, pick)
        got = got[:width] + got[width : 2 * width] + got[2 * width :]
        out = got if out is None else out + got
    out_ref[...] = out


def first_kernel(dofs_ref, stiff_ref, proj_ref, star_ref, send_ref,
                 first_ref, second_ref, faces_ref, bh_ref, bl_ref, x0_ref, out_ref, rows_ref,
                 stiff_form_ref, face_form_ref):
    var_count, _, dims, elem_count = star_ref.shape
    face_count = proj_ref.shape[1]
    cols = var_count * elem_count
    x = dofs_ref[...].T
    x0_ref[...] = x
    lane = lax.broadcasted_iota(jnp.int32, (elem_count, cols), 1) % elem_count
    keep = lane == lax.broadcasted_iota(jnp.int32, (elem_count, cols), 0)
    flats = [
        jnp.concatenate([star_ref[v, w] for v in range(var_count)], axis=1)
        for w in range(var_count)
    ]
    for d in range(dims):
        b = jnp.concatenate(
            [
                jnp.where(keep, jnp.broadcast_to(flats[w][d : d + 1], (elem_count, cols)), 0.0)
                for w in range(var_count)
            ],
            axis=0,
        )
        hi, lo = halves(b)
        bh_ref[d] = hi.astype(bf16)
        bl_ref[d] = lo.astype(bf16)
    form = left_form(stiff_rows(stiff_ref, False))
    stiff_form_ref[...] = form
    first, second = series(
        form, x, bh_ref, bl_ref,
        [taylor_weights(0.0, fine_step, ORDER), taylor_weights(fine_step, 2.0 * fine_step, ORDER)],
    )
    first_ref[...] = first
    second_ref[...] = second
    rows_all = face_rows(proj_ref)
    rows_ref[...] = rows_all
    face_form = left_form(rows_all)
    face_form_ref[...] = face_form
    faces_all = left(face_form, first)
    faces_ref[...] = faces_all
    export_rows(faces_all, send_ref, out_ref, var_count, elem_count, face_count)


def own_terms(base, x, faces_all, flip_form_ref, surface_form_ref, bh_ref, bl_ref, ch_ref, cl_ref):
    face_count = ch_ref.shape[0]
    width = faces_all.shape[0] // face_count
    volume = star_apply(flip_form_ref[...], x, bh_ref, bl_ref)
    wide = jnp.concatenate(
        [faces_all[f * width : (f + 1) * width] for f in range(face_count)], axis=1
    )
    flux = jnp.concatenate(
        [right(wide, ch_ref[f], cl_ref[f]) for f in range(face_count)], axis=0
    )
    return base + volume - left(surface_form_ref[...], flux)


def matrices_kernel(minus_ref, plus_ref, fault_flux_ref, fault_ref, source_ref, stiff_ref,
                    rows_ref, sub_ref, ch_ref, cl_ref, rh_ref, rl_ref, flip_form_ref,
                    surface_form_ref, *, sub_count, slots):
    var_count, _, face_count, elem_count = minus_ref.shape
    flip_form_ref[...] = left_form(stiff_rows(stiff_ref, True))
    surface_form_ref[...] = left_form(rows_ref[...].T)
    cols = var_count * elem_count
    lane = lax.broadcasted_iota(jnp.int32, (elem_count, cols), 1) % elem_count
    row = lax.broadcasted_iota(jnp.int32, (elem_count, cols), 0)
    keep = lane == row
    eye = (
        lax.broadcasted_iota(jnp.int32, (var_count, var_count), 0)
        == lax.broadcasted_iota(jnp.int32, (var_count, var_count), 1)
    )
    fault_flux = fault_flux_ref[...]
    columns = []
    for v in range(var_count):
        line = jnp.broadcast_to(fault_flux[v : v + 1], (var_count, var_count))
        column = jnp.sum(jnp.where(eye, line, 0.0), axis=1, keepdims=True)
        columns.append(jnp.broadcast_to(column, (var_count, elem_count)))
    friction = jnp.concatenate(columns, axis=1)
    own_sub = sub_ref[0]
    group = var_count * slots
    rslot = lax.broadcasted_iota(jnp.int32, (group, cols), 0) % slots
    sources = jnp.concatenate([source_ref[...]] * var_count, axis=1)
    faults = jnp.concatenate([fault_ref[...]] * var_count, axis=1)
    couples, minuses = [], []
    for w in range(var_count):
        plus = jnp.concatenate([plus_ref[v, w] for v in range(var_count)], axis=1)
        minuses.append(jnp.concatenate([minus_ref[v, w] for v in range(var_count)], axis=1))
        couples.append(jnp.where(faults == 1, friction[w : w + 1], plus))
    for f in range(face_count):
        source = sources[f : f + 1]
        for g in range(face_count):
            match = (source - g * elem_count) == row
            blocks = []
            for w in range(var_count):
                block = jnp.where(match, couples[w][f : f + 1], 0.0)
                if g == f:
                    block = block + jnp.where(keep, minuses[w][f : f + 1], 0.0)
                blocks.append(block)
            hi, lo = halves(jnp.concatenate(blocks, axis=0))
            ch_ref[f, g * cols : (g + 1) * cols] = hi.astype(bf16)
            cl_ref[f, g * cols : (g + 1) * cols] = lo.astype(bf16)
        grown = jnp.concatenate(
            [jnp.broadcast_to(c[f : f + 1], (slots, cols)) for c in couples], axis=0
        )
        pieces = []
        for side in range(3):
            for delta in range(sub_count):
                place = (own_sub + delta) % sub_count
                start = face_count * elem_count + (side * sub_count + place) * slots
                pieces.append(jnp.where((source - start) == rslot, grown, 0.0))
        hi, lo = halves(jnp.concatenate(pieces, axis=0))
        rh_ref[f] = hi.astype(bf16)
        rl_ref[f] = lo.astype(bf16)


def remote_terms(acc_ref, message_refs, rh_ref, rl_ref, surface_form_ref):
    width = surface_form_ref.shape[1] // (3 * rh_ref.shape[0])
    wide = jnp.concatenate(
        [m[k : k + width] for m in message_refs for k in range(0, m.shape[0], width)], axis=1
    )
    flux = jnp.concatenate(
        [right(wide, rh_ref[f], rl_ref[f]) for f in range(rh_ref.shape[0])], axis=0
    )
    return acc_ref[...] - left(surface_form_ref[...], flux)


def middle_kernel(acc_ref, rh_ref, rl_ref, stiff_form_ref, face_form_ref, surface_form_ref, bh_ref, bl_ref, second_ref,
                  levels_ref, send_ref, *rest):
    message_refs, (moved_ref, carried_ref, faces_ref, out_ref) = rest[:-4], rest[-4:]
    elem_count = levels_ref.shape[1]
    var_count = acc_ref.shape[1] // elem_count
    moved = remote_terms(acc_ref, message_refs, rh_ref, rl_ref, surface_form_ref)
    moved_ref[...] = moved
    form = stiff_form_ref[...]
    (fine,) = series(form, moved, bh_ref, bl_ref, [taylor_weights(0.0, fine_step, ORDER)])
    levels = jnp.concatenate([levels_ref[...]] * var_count, axis=1)
    carried = jnp.where(levels == 0, fine, second_ref[...])
    carried_ref[...] = carried
    faces_all = left(face_form_ref[...], carried)
    faces_ref[...] = faces_all
    export_rows(faces_all, send_ref, out_ref, var_count, elem_count, rh_ref.shape[0])


def own_kernel(base_ref, x_ref, faces_ref, flip_form_ref, surface_form_ref, bh_ref, bl_ref,
               ch_ref, cl_ref, acc_ref):
    acc_ref[...] = own_terms(base_ref[...], x_ref[...], faces_ref[...], flip_form_ref,
                             surface_form_ref, bh_ref, bl_ref, ch_ref, cl_ref)


def last_kernel(acc_ref, rh_ref, rl_ref, surface_form_ref, *rest):
    message_refs, out_ref = rest[:-1], rest[-1]
    out_ref[...] = remote_terms(acc_ref, message_refs, rh_ref, rl_ref, surface_form_ref).T


def exchange(message):
    dom_count, sub_count = lax.axis_size("dom"), lax.axis_size("sub")
    group = [message]
    for delta in range(1, sub_count):
        pairs = [((sub + delta) % sub_count, sub) for sub in range(sub_count)]
        group.append(lax.ppermute(message, "sub", pairs))
    group = jnp.concatenate(group, axis=0)
    up = [(i, (i + 1) % dom_count) for i in range(dom_count)]
    down = [(j, i) for i, j in up]
    return [lax.ppermute(group, "dom", up), group, lax.ppermute(group, "dom", down)]


def pin(x):
    return pltpu.with_memory_space_constraint(x, pltpu.VMEM)


def call(kernel, places, shapes, *operands, cost=None):
    vmem = pl.BlockSpec(memory_space=pltpu.VMEM)
    spec = {"p": vmem, "v": vmem, "s": pl.BlockSpec(memory_space=pltpu.SMEM)}
    outs = [
        pltpu.VMEM(shape[0], shape[1]) if len(shape) > 2 else jax.ShapeDtypeStruct(*shape)
        for shape in shapes
    ]
    single = len(outs) == 1
    return pl.pallas_call(
        kernel,
        in_specs=[spec[p] for p in places],
        out_specs=vmem if single else [vmem] * len(outs),
        out_shape=outs[0] if single else outs,
        cost_estimate=cost,
    )(*[pin(x) if p == "p" else x for p, x in zip(places, operands)])


def per_device(
    dofs,
    stiffness,
    projection,
    star,
    flux_minus,
    flux_plus,
    fault_flux,
    fault_faces,
    levels,
    face_source,
    send_source,
):
    var_count, modes, elem_count = dofs.shape
    face_count, face_modes, _ = projection.shape
    dims = stiffness.shape[0]
    slots = send_source.shape[0]
    sub_count = lax.axis_size("sub")
    cols = var_count * elem_count
    width = face_pad(face_modes)
    field = ((modes, cols), f32, True)
    faces_shape = ((face_count * width, cols), f32, True)
    block = ((dims, cols, cols), bf16, True)
    sent = ((width, var_count * slots), f32, True)
    local = ((face_count, face_count * cols, cols), bf16)
    remote = ((face_count, 3 * sub_count * var_count * slots, cols), bf16, True)
    sub_index = lax.axis_index("sub").reshape(1).astype(jnp.int32)
    levels_row = levels.reshape(1, elem_count)
    work = pl.CostEstimate(flops=400_000_000, bytes_accessed=4_000_000, transcendentals=0)

    dofs_view = jnp.transpose(dofs, (0, 2, 1)).reshape(cols, modes)
    star_view = jnp.transpose(star, (1, 2, 0, 3))
    minus_view = jnp.transpose(flux_minus, (1, 2, 0, 3))
    plus_view = jnp.transpose(flux_plus, (1, 2, 0, 3))
    projection_view = jnp.transpose(projection, (1, 0, 2))
    first, second, faces_first, bh, bl, x0, message, rows, stiff_form, face_form = call(
        first_kernel, "vvvvs",
        [field, field, faces_shape, block, block, field, sent, ((face_count * width, modes), f32, True),
         ((dims * modes, 3 * modes), bf16, True), ((face_count * width, 3 * modes), bf16, True)],
        dofs_view, stiffness, projection_view, star_view, send_source,
    )
    got = exchange(message)
    ch, cl, rh, rl, flip_form, surface_form = call(
        lambda *refs: matrices_kernel(*refs, sub_count=sub_count, slots=slots),
        "v" * 6 + "ps",
        [local, local, remote, remote, ((dims * modes, 3 * modes), bf16, True),
         ((modes, 3 * face_count * width), bf16, True)],
        minus_view, plus_view, fault_flux, fault_faces, face_source, stiffness, rows, sub_index, cost=work,
    )
    acc = call(
        own_kernel, "pppppppvv", [field],
        x0, first, faces_first, flip_form, surface_form, bh, bl, ch, cl, cost=work,
    )
    count = len(got)
    moved, carried, faces_carried, message = call(
        middle_kernel, "ppppppppp" + "vs" + "p" * count, [field, field, faces_shape, sent],
        acc, rh, rl, stiff_form, face_form, surface_form, bh, bl, second, levels_row, send_source, *got,
    )
    got = exchange(message)
    acc = call(
        own_kernel, "pppppppvv", [field],
        moved, carried, faces_carried, flip_form, surface_form, bh, bl, ch, cl, cost=work,
    )
    out = call(
        last_kernel, "pppp" + "p" * count, [((cols, modes), f32)],
        acc, rh, rl, surface_form, *got,
    )
    return jnp.transpose(out.reshape(var_count, elem_count, modes), (0, 2, 1))


def solution(mesh):
    return jax.shard_map(
        per_device,
        mesh=mesh,
        in_specs=(
            P(None, None, ("dom", "sub")),
            P(),
            P(),
            P(None, None, None, ("dom", "sub")),
            P(None, None, None, ("dom", "sub")),
            P(None, None, None, ("dom", "sub")),
            P(),
            P(None, ("dom", "sub")),
            P(("dom", "sub")),
            P(None, ("dom", "sub")),
            P(("dom", "sub")),
        ),
        out_specs=P(None, None, ("dom", "sub")),
        check_vma=False,
    )
```
